128 devices in a mesh: grp: 16 (over y, x), lag: 8 (over z, core).
Axes of the slice: x: 4, y: 4, z: 4, core: 2. Of those that a mesh axis runs over, the one named last changes fastest.
Arguments:
- weights: bfloat16 [3, 16384, 256], P(None, 'lag'), may hold values from -0.125 to 0.125
- history: bfloat16 [512, 2048, 256], P(('grp', 'lag')), may hold values from -6 to 6
- send_patch: int32 [2048, 2], P(('grp', 'lag')), may hold values from 0 to 3
- send_lag: int32 [2048, 2], P(('grp', 'lag')), may hold values from 0 to 56
- send_class: int32 [2048, 2], P(('grp', 'lag')), may hold values from 0 to 2
- recv_target: int32 [2048, 2], P(('grp', 'lag')), may hold values from 0 to 3
- local_src: int32 [6144], P(('grp', 'lag')), may hold values from 0 to 3
- local_lag: int32 [6144], P(('grp', 'lag')), may hold values from 0 to 56
- local_class: int32 [6144], P(('grp', 'lag')), may hold values from 0 to 2
- local_target: int32 [6144], P(('grp', 'lag')), may hold values from 0 to 3
- inverse_blocks: bfloat16 [512, 256, 256], P(('grp', 'lag')), may hold values from -0.375 to 0.375
- incident: bfloat16 [512, 256, 256], P(('grp', 'lag')), may hold values from -6 to 6
Outputs:
- density: bfloat16 [512, 256, 256], P(('grp', 'lag'))
The draws below stay inside these ranges and needn't reach their ends.
All inputs are finite; a program needn't handle non-finite values.
Results may differ from the reference program's by a relative error of at most 0.0049.
Values may be sent and summed in bfloat16 or wider, within the bound.
A program may use at most 256 MiB of HBM per device.

```python
import jax
import jax.numpy as jnp
from jax import lax

P_SIZE = 256
C = 256
M = 8
LAGS = 64
CLASSES = 3
PD = 4
CAP = 2
NLOC = 48
PATCHES = 512
N_GRP = 16
N_LAG = 8


def with_ends(values, rng, smallest, top_value):
    place = [jax.random.randint(jax.random.fold_in(rng, axis), (), 0, length) for axis, length in enumerate(values.shape)]
    main_axis = values.shape.index(max(values.shape))
    beside = place[:main_axis] + [(place[main_axis] + 1) % values.shape[main_axis]] + place[main_axis + 1:]
    return values.at[tuple(place)].set(smallest).at[tuple(beside)].set(top_value)


def levels(key, shape, cuts, smallest, top_value):
    gain, own = 1.0, jax.random.fold_in(key, 6)
    for position, blocks in cuts:
        heights = jnp.exp(jax.random.uniform(jax.random.fold_in(own, position), (blocks,), jnp.float32, smallest / len(cuts), top_value / len(cuts)))
        gain = gain * jnp.repeat(heights, shape[position] // blocks).reshape([-1 if axis == position else 1 for axis in range(len(shape))])
    return gain


def gaussian(own_key, dims, spread, reach, shards=(), kind=jnp.bfloat16):
    array = jax.random.normal(own_key, dims, jnp.float32) * spread
    if len(shards) > 0:
        array = levels(own_key, dims, shards, -0.22, 0.18) * array
    return jnp.clip(array, min=-reach, max=reach).astype(kind)


def setup_inputs(seed: int = 0) -> dict:
    keys = jax.random.split(jax.random.key(seed), 13)
    weights = gaussian(keys[0], (CLASSES, LAGS * P_SIZE, P_SIZE), (M * P_SIZE) ** -0.5, 0.125, ((1, 8),))
    history = gaussian(keys[1], (PATCHES, M * P_SIZE, C), 1.0, 6.0, ((0, 128),))
    send_patch = with_ends(jax.random.randint(keys[2], (N_GRP * N_LAG * N_GRP, CAP), 0, PD), jax.random.fold_in(keys[2], 1), 0, PD - 1).astype(jnp.int32)
    send_lag = with_ends(jax.random.randint(keys[3], (N_GRP * N_LAG * N_GRP, CAP), 0, LAGS - M + 1), jax.random.fold_in(keys[3], 1), 0, LAGS - M).astype(jnp.int32)
    send_class = with_ends(jax.random.randint(keys[4], (N_GRP * N_LAG * N_GRP, CAP), 0, CLASSES), jax.random.fold_in(keys[4], 1), 0, CLASSES - 1).astype(jnp.int32)
    recv_target = with_ends(jax.random.randint(keys[5], (N_GRP * N_LAG * N_GRP, CAP), 0, PD), jax.random.fold_in(keys[5], 1), 0, PD - 1).astype(jnp.int32)
    local_src = with_ends(jax.random.randint(keys[6], (N_GRP * N_LAG * NLOC,), 0, PD), jax.random.fold_in(keys[6], 1), 0, PD - 1).astype(jnp.int32)
    local_lag = with_ends(jax.random.randint(keys[7], (N_GRP * N_LAG * NLOC,), 0, LAGS - M + 1), jax.random.fold_in(keys[7], 1), 0, LAGS - M).astype(jnp.int32)
    local_class = with_ends(jax.random.randint(keys[8], (N_GRP * N_LAG * NLOC,), 0, CLASSES), jax.random.fold_in(keys[8], 1), 0, CLASSES - 1).astype(jnp.int32)
    local_target = with_ends(jax.random.randint(keys[9], (N_GRP * N_LAG * NLOC,), 0, PD), jax.random.fold_in(keys[9], 1), 0, PD - 1).astype(jnp.int32)
    inverse_blocks = gaussian(keys[10], (PATCHES, P_SIZE, P_SIZE), P_SIZE ** -0.5, 0.375, ((0, 128),))
    incident = gaussian(keys[11], (PATCHES, P_SIZE, C), 1.0, 6.0, ((0, 128),))
    return dict(weights=weights, history=history, send_patch=send_patch, send_lag=send_lag, send_class=send_class, recv_target=recv_target, local_src=local_src, local_lag=local_lag, local_class=local_class, local_target=local_target, inverse_blocks=inverse_blocks, incident=incident)


def pair_blocks(weights_full, hist_rows, classes, offsets):
    def window(klass, offset):
        return lax.dynamic_slice(weights_full, (klass, offset * P_SIZE, jnp.int32(0)), (1, M * P_SIZE, P_SIZE))[0]
    blocks = jax.vmap(window)(classes.astype(jnp.int32), offsets.astype(jnp.int32))
    return jnp.einsum("bkp,bkc->bpc", blocks, hist_rows, precision=lax.Precision.HIGHEST)


def reference(weights, history, send_patch, send_lag, send_class, recv_target, local_src, local_lag, local_class, local_target, inverse_blocks, incident):
    devices = N_GRP * N_LAG
    weights_full = weights.astype(jnp.float32)
    owner = jnp.arange(devices, dtype=jnp.int32)
    local_s = (owner[:, None] * PD + local_src.reshape(devices, NLOC)).astype(jnp.int32)
    local_o = local_lag.reshape(devices, NLOC).astype(jnp.int32)
    local_k = local_class.reshape(devices, NLOC).astype(jnp.int32)
    local_t = (owner[:, None] * PD + local_target.reshape(devices, NLOC)).astype(jnp.int32)
    sender = owner.reshape(N_GRP, N_LAG, 1, 1)
    peer_grp = jnp.arange(N_GRP, dtype=jnp.int32).reshape(1, 1, N_GRP, 1)
    lane_idx = jnp.arange(N_LAG, dtype=jnp.int32).reshape(1, N_LAG, 1, 1)
    remote_s = sender * PD + send_patch.reshape(N_GRP, N_LAG, N_GRP, CAP)
    remote_o = send_lag.reshape(N_GRP, N_LAG, N_GRP, CAP)
    remote_k = send_class.reshape(N_GRP, N_LAG, N_GRP, CAP)
    targets_back = jnp.transpose(recv_target.reshape(N_GRP, N_LAG, N_GRP, CAP), (2, 1, 0, 3))
    remote_t = (peer_grp * N_LAG + lane_idx) * PD + targets_back
    all_s = jnp.concatenate([local_s, remote_s.reshape(devices, N_GRP * CAP).astype(jnp.int32)], 1)
    all_o = jnp.concatenate([local_o, remote_o.reshape(devices, N_GRP * CAP).astype(jnp.int32)], 1)
    all_k = jnp.concatenate([local_k, remote_k.reshape(devices, N_GRP * CAP).astype(jnp.int32)], 1)
    all_t = jnp.concatenate([local_t, remote_t.reshape(devices, N_GRP * CAP).astype(jnp.int32)], 1)

    def advance(near_sum, inputs):
        sources, classes, offsets, targets = inputs
        hist_rows = history[sources].astype(jnp.float32)
        contrib = pair_blocks(weights_full, hist_rows, classes, offsets)
        return near_sum.at[targets].add(contrib), None

    near0 = jnp.zeros((history.shape[0], P_SIZE, C), jnp.float32)
    near_sum, _ = lax.scan(advance, near0, (all_s, all_k, all_o, all_t))
    residual = (incident.astype(jnp.float32) - near_sum).astype(jnp.bfloat16)
    density = jnp.einsum("tpq,tqc->tpc", inverse_blocks.astype(jnp.float32), residual.astype(jnp.float32), precision=lax.Precision.HIGHEST)
    return density.astype(jnp.bfloat16)
```

```python
import jax
import jax.numpy as jnp
from jax import lax
from jax.experimental import pallas as pl
from jax.experimental.pallas import tpu as pltpu
from jax.sharding import PartitionSpec as P

MESH = pl.DeviceIdType.MESH
PANEL = 256
STEPS = 8
LAGS = 64
OWN_LAGS = 8
CLASSES = 3
OWNED = 4
SIDE = 4
SLOTS = 2
NLOC = 48
GROUP = 8


def near_kernel(
    w_hbm, h_hbm, send_patch, send_lag, send_class, recv_target,
    local_src, local_lag, local_class, local_target,
    near_ref,
    table, hist_t, hist_in, send_buf, recv_buf, merged, arrived, contrib, target_own, target_row,
    send_sem, recv_sem, pair_send, pair_recv, load_sem, hist_sem,
):
    grp = lax.axis_index("grp")
    lag = lax.axis_index("lag")
    core = lax.rem(lag, 2)
    zpos = lag // 2
    xpos = lax.rem(grp, SIDE)
    ypos = grp // SIDE
    a_pos = jnp.where(core == 0, xpos, ypos)
    b_pos = jnp.where(core == 0, ypos, xpos)
    a_unit = jnp.where(core == 0, 1, SIDE)
    b_unit = jnp.where(core == 0, SIDE, 1)

    def at(pos, step):
        return lax.rem(pos + step, SIDE)

    def device(da=0, db=0, dz=0):
        return (at(a_pos, da) * a_unit + at(b_pos, db) * b_unit, at(zpos, dz) * 2 + core)

    twin = (grp, zpos * 2 + 1 - core)

    sizes = []

    def send(src, dst, to):
        n = len(sizes)
        sizes.append(src)
        pltpu.make_async_remote_copy(
            src_ref=src, dst_ref=dst, send_sem=send_sem.at[n], recv_sem=recv_sem.at[n],
            device_id=to, device_id_type=MESH,
        ).start()
        return n

    def arrive(n, ref):
        pltpu.make_async_remote_copy(
            src_ref=ref, dst_ref=ref, send_sem=send_sem.at[n], recv_sem=recv_sem.at[n],
            device_id=twin, device_id_type=MESH,
        ).wait_recv()

    def sent(n, ref):
        pltpu.make_async_remote_copy(
            src_ref=ref, dst_ref=ref, send_sem=send_sem.at[n], recv_sem=recv_sem.at[n],
            device_id=twin, device_id_type=MESH,
        ).wait_send()

    def shard(dz, c=None):
        return at(zpos, dz) * 2 + (core if c is None else c)

    def direct(dz, half=None, c=None):
        start = shard(dz, c) * OWN_LAGS
        if half is None:
            return table.at[pl.ds(start, 8)]
        return table.at[pl.ds(start + 4 * half, 4)]

    def one(dz, da):
        s = b_pos * SIDE + at(a_pos, da)
        return table.at[pl.ds((1 + s // 8) * LAGS + shard(dz) * OWN_LAGS + lax.rem(s, 8), 1)]

    def row(dz, db, half=None, bb=None, c=None):
        b = at(b_pos, db) if bb is None else bb
        start = (1 + b // 2) * LAGS + shard(dz, c) * OWN_LAGS + lax.rem(b, 2) * 4
        if half is None:
            return table.at[pl.ds(start, 4)]
        return table.at[pl.ds(start + 2 * half, 2)]

    loads = [
        pltpu.make_async_copy(
            w_hbm.at[pl.ds(k * OWN_LAGS, OWN_LAGS)],
            table.at[pl.ds(k * LAGS + lag * OWN_LAGS, OWN_LAGS)],
            load_sem.at[k],
        )
        for k in range(CLASSES)
    ]
    hist = [
        pltpu.make_async_copy(h_hbm.at[s], hist_in.at[s % 2], hist_sem.at[s]) for s in range(OWNED)
    ]
    hist[0].start()
    hist[1].start()

    barrier = pltpu.get_barrier_semaphore()
    partners = [twin]
    for d in (1, 2, 3):
        partners += [device(da=d), device(db=d), device(dz=d)]
    for p in partners:
        pl.semaphore_signal(barrier, inc=1, device_id=p, device_id_type=MESH)

    for b in range(SIDE):
        for a in range(SIDE):
            for s in range(SLOTS):
                value = recv_target[a * a_unit + b * b_unit, s]
                target_own[b, pl.ds(a * SLOTS + s, 1), :] = jnp.full((1, PANEL), value, jnp.int32)
    target_row[3] = target_own[b_pos]
    pl.semaphore_wait(barrier, len(partners))

    own = b_pos * SIDE + a_pos
    slice_id = {}
    for dz in (1, 3, 2):
        slice_id[dz] = send(w_hbm.at[pl.ds(8 + own, 1)], one(0, 0), device(dz=dz))
    direct_id = {}
    for first in (True, False):
        for dz in (1, 3):
            half = (0 if dz == 1 else 1) if first else (1 if dz == 1 else 0)
            direct_id[dz, half] = send(w_hbm.at[pl.ds(4 * half, 4)], direct(0, half), device(dz=dz))
    target_id = {}
    for dd in (1, 2, 3):
        target_id[3 - dd] = send(target_own.at[at(b_pos, dd)], target_row.at[3 - dd], device(db=dd))
    for copy in loads:
        copy.start()
    twin_in = []
    for k in range(CLASSES):
        n = send(
            w_hbm.at[pl.ds(k * OWN_LAGS, OWN_LAGS)],
            table.at[pl.ds(k * LAGS + lag * OWN_LAGS, OWN_LAGS)],
            twin,
        )
        twin_in.append((n, table.at[pl.ds(k * LAGS + shard(0, 1 - core) * OWN_LAGS, OWN_LAGS)]))

    def turn(s):
        hist[s].wait()

        @pl.loop(0, STEPS)
        def _(m):
            block = hist_in[s % 2, pl.ds(pl.multiple_of(m * PANEL, PANEL), PANEL), :]
            hist_t[s, :, pl.ds(pl.multiple_of(m * PANEL, PANEL), PANEL)] = block.T

    turn(0)
    hist[2].start()
    turn(1)
    hist[3].start()

    first_id = {}
    for dz in (1, 3, 2):
        arrive(slice_id[dz], one(-dz % 4, 0))
        for da in (1, 3, 2):
            first_id[dz, da] = send(one(-dz % 4, 0), one(-dz % 4, 0), device(da=da))
    turn(2)
    turn(3)
    zero = jnp.zeros((PANEL, PANEL), jnp.float32)
    for t in range(OWNED):
        near_ref[t] = zero

    second_id = {}
    for dz in (1, 3, 2):
        for da in (1, 3, 2):
            arrive(first_id[dz, da], one(-dz % 4, -da % 4))
        for db, half in ((1, 0), (3, 1), (1, 1), (3, 0)):
            second_id[dz, db, half] = send(row(-dz % 4, 0, half), row(-dz % 4, 0, half), device(db=db))
        n = send(row(-dz % 4, 0), row(-dz % 4, 0), twin)
        twin_in.append((n, row(-dz % 4, 0, bb=jnp.where(core == 0, xpos, ypos), c=1 - core)))

    relay_id = {}
    for dz, half in ((1, 0), (3, 1)):
        arrive(direct_id[dz, half], direct(-dz % 4, half))
        relay_id[dz] = send(direct(-dz % 4, half), direct(-dz % 4, half), device(dz=dz))
    for dz, half in ((1, 1), (3, 0)):
        arrive(direct_id[dz, half], direct(-dz % 4, half))
        n = send(direct(-dz % 4), direct(-dz % 4), twin)
        twin_in.append((n, direct(-dz % 4, c=1 - core)))

    pass_id = {}
    for dz in (1, 3, 2):
        for db, half in ((1, 0), (3, 1)):
            arrive(second_id[dz, db, half], row(-dz % 4, -db % 4, half))
            pass_id[dz, db] = send(row(-dz % 4, -db % 4, half), row(-dz % 4, -db % 4, half), device(db=db))
        for db, half in ((1, 1), (3, 0)):
            arrive(second_id[dz, db, half], row(-dz % 4, -db % 4, half))
            n = send(row(-dz % 4, -db % 4), row(-dz % 4, -db % 4), twin)
            other = at(a_pos, -db % 4)
            twin_in.append((n, row(-dz % 4, 0, bb=other, c=1 - core)))
    for dz, half in ((1, 0), (3, 1)):
        arrive(relay_id[dz], direct(2, half))
    n = send(direct(2), direct(2), twin)
    twin_in.append((n, direct(2, c=1 - core)))
    for dz in (1, 3, 2):
        for db, half in ((1, 0), (3, 1)):
            arrive(pass_id[dz, db], row(-dz % 4, 2, half))
        n = send(row(-dz % 4, 2), row(-dz % 4, 2), twin)
        twin_in.append((n, row(-dz % 4, 0, bb=at(a_pos, 2), c=1 - core)))
    for n, ref in twin_in:
        arrive(n, ref)
    for copy in loads:
        copy.wait()

    def product(klass, offset, patch):
        window = table[pl.ds(klass * LAGS + offset, STEPS)].reshape(STEPS * PANEL, PANEL)
        return jnp.dot(hist_t[patch], window, preferred_element_type=jnp.float32)

    def pair_copy(q):
        da = lax.rem(lax.rem(q, 4) + 1, 4)
        return pltpu.make_async_remote_copy(
            src_ref=send_buf.at[pl.ds(q * SLOTS, SLOTS)], dst_ref=recv_buf.at[pl.ds(q * SLOTS, SLOTS)],
            send_sem=pair_send.at[q], recv_sem=pair_recv.at[q],
            device_id=device(da=da), device_id_type=MESH,
        )

    @pl.loop(0, SIDE * SIDE)
    def _(q):
        db = q // 4
        da = lax.rem(lax.rem(q, 4) + 1, 4)
        peer = at(a_pos, da) * a_unit + at(b_pos, db + 1) * b_unit
        for s in range(SLOTS):
            block = product(send_class[peer, s], send_lag[peer, s], send_patch[peer, s])
            send_buf[q * SLOTS + s] = block.astype(jnp.bfloat16)

        @pl.when(da != 0)
        def _():
            pair_copy(q).start()

    def local(first, count):
        @pl.loop(first, first + count)
        def _(group):
            @pl.loop(0, GROUP)
            def _(i):
                j = group * GROUP + i
                contrib[i] = product(local_class[j], local_lag[j], local_src[j])

            @pl.loop(0, PANEL // 8)
            def _(chunk):
                rows = pl.ds(pl.multiple_of(chunk * 8, 8), 8)
                parts = [contrib[i, rows, :] for i in range(GROUP)]
                for t in range(OWNED):
                    total = near_ref[t, rows, :]
                    for i in range(GROUP):
                        total += jnp.where(local_target[group * GROUP + i] == t, parts[i], 0.0)
                    near_ref[t, rows, :] = total

    def merge(db):
        for r in range(3):
            pair_copy(db * 4 + r).wait_recv()

        @pl.loop(0, PANEL // 16)
        def _(chunk):
            rows = pl.ds(pl.multiple_of(chunk * 16, 16), 16)
            totals = [None] * OWNED
            for r in range(4):
                da = (r + 1) % 4
                source = at(a_pos, -da % 4)
                buffer = send_buf if da == 0 else recv_buf
                for s in range(SLOTS):
                    part = buffer[(db * 4 + r) * SLOTS + s, rows, :].astype(jnp.float32)
                    which = target_row[db, pl.ds(source * SLOTS + s, 1), :]
                    for t in range(OWNED):
                        kept = jnp.where(jnp.broadcast_to(which, part.shape) == t, part, 0.0)
                        totals[t] = kept if totals[t] is None else totals[t] + kept
            for t in range(OWNED):
                if db < 3:
                    merged[db * OWNED + t, rows, :] = totals[t].astype(jnp.bfloat16)
                else:
                    near_ref[t, rows, :] += totals[t]

    def merged_copy(db):
        return pltpu.make_async_remote_copy(
            src_ref=merged.at[pl.ds(db * OWNED, OWNED)], dst_ref=arrived.at[pl.ds(db * OWNED, OWNED)],
            send_sem=pair_send.at[16 + db], recv_sem=pair_recv.at[16 + db],
            device_id=device(db=db + 1), device_id_type=MESH,
        )

    for db in range(3):
        arrive(target_id[db], target_row.at[db])
    for db in range(3):
        merge(db)
        merged_copy(db).start()
        local(2 * db, 2)
    merge(3)
    for db in range(3):
        merged_copy(db).wait_recv()

    @pl.loop(0, PANEL // 16)
    def _(chunk):
        rows = pl.ds(pl.multiple_of(chunk * 16, 16), 16)
        for t in range(OWNED):
            total = near_ref[t, rows, :]
            for db in range(3):
                total += arrived[db * OWNED + t, rows, :].astype(jnp.float32)
            near_ref[t, rows, :] = total

    for db in range(4):
        for r in range(3):
            pair_copy(db * 4 + r).wait_send()
    for db in range(3):
        merged_copy(db).wait_send()
    for n, ref in enumerate(sizes):
        sent(n, ref)


def near_field(weights, history, tables):
    vmem = pltpu.VMEM
    smem = pl.BlockSpec(memory_space=pltpu.SMEM)
    anywhere = pl.BlockSpec(memory_space=pl.ANY)
    return pl.pallas_call(
        near_kernel,
        out_shape=jax.ShapeDtypeStruct((OWNED, PANEL, PANEL), jnp.float32),
        in_specs=[anywhere, anywhere] + [smem] * 8,
        out_specs=pl.BlockSpec(memory_space=vmem),
        scratch_shapes=[
            vmem((CLASSES * LAGS, PANEL, PANEL), jnp.bfloat16),
            vmem((OWNED, PANEL, STEPS * PANEL), jnp.bfloat16),
            vmem((2, STEPS * PANEL, PANEL), jnp.bfloat16),
            vmem((32, PANEL, PANEL), jnp.bfloat16),
            vmem((32, PANEL, PANEL), jnp.bfloat16),
            vmem((12, PANEL, PANEL), jnp.bfloat16),
            vmem((12, PANEL, PANEL), jnp.bfloat16),
            vmem((GROUP, PANEL, PANEL), jnp.float32),
            vmem((SIDE, SIDE * SLOTS, PANEL), jnp.int32),
            vmem((SIDE, SIDE * SLOTS, PANEL), jnp.int32),
            pltpu.SemaphoreType.DMA((80,)),
            pltpu.SemaphoreType.DMA((80,)),
            pltpu.SemaphoreType.DMA((19,)),
            pltpu.SemaphoreType.DMA((19,)),
            pltpu.SemaphoreType.DMA((CLASSES,)),
            pltpu.SemaphoreType.DMA((OWNED,)),
        ],
        compiler_params=pltpu.CompilerParams(
            collective_id=0, has_side_effects=True, vmem_limit_bytes=60 * 2**20
        ),
    )(weights.reshape(CLASSES * OWN_LAGS, PANEL, PANEL), history, *tables)


def per_device(
    weights, history, send_patch, send_lag, send_class, recv_target,
    local_src, local_lag, local_class, local_target, inverse_blocks, incident,
):
    near_t = near_field(
        weights, history,
        (send_patch, send_lag, send_class, recv_target, local_src, local_lag, local_class, local_target),
    )
    near_sum = jnp.swapaxes(near_t, 1, 2)
    residual = (incident.astype(jnp.float32) - near_sum).astype(jnp.bfloat16)
    density = jnp.einsum("tpq,tqc->tpc", inverse_blocks, residual, preferred_element_type=jnp.float32)
    return density.astype(jnp.bfloat16)


def solution(mesh):
    both = ("grp", "lag")
    return jax.shard_map(
        per_device,
        mesh=mesh,
        in_specs=(
            P(None, "lag", None), P(both, None, None),
            P(both, None), P(both, None), P(both, None), P(both, None),
            P(both), P(both), P(both), P(both),
            P(both, None, None), P(both, None, None),
        ),
        out_specs=P(both, None, None),
        check_vma=False,
    )
```

```python
import jax
import jax.numpy as jnp
from jax import lax
from jax.experimental import pallas as pl
from jax.experimental.pallas import tpu as pltpu
from jax.sharding import PartitionSpec as P

MESH = pl.DeviceIdType.MESH
PANEL = 256
STEPS = 8
LAGS = 64
OWN_LAGS = 8
CLASSES = 3
OWNED = 4
SIDE = 4
SLOTS = 2
NLOC = 48
GROUP = 8


def near_kernel(
    w_hbm, h_hbm, send_patch, send_lag, send_class, recv_target,
    local_src, local_lag, local_class, local_target,
    near_ref,
    table, hist_t, hist_in, send_buf, recv_buf, merged, arrived, contrib, target_own, target_row,
    send_sem, recv_sem, pair_send, pair_recv, load_sem, hist_sem,
):
    grp = lax.axis_index("grp")
    lag = lax.axis_index("lag")
    core = lax.rem(lag, 2)
    zpos = lag // 2
    xpos = lax.rem(grp, SIDE)
    ypos = grp // SIDE
    a_pos = jnp.where(core == 0, xpos, ypos)
    b_pos = jnp.where(core == 0, ypos, xpos)
    a_unit = jnp.where(core == 0, 1, SIDE)
    b_unit = jnp.where(core == 0, SIDE, 1)

    def at(pos, step):
        return lax.rem(pos + step, SIDE)

    def device(da=0, db=0, dz=0):
        return (at(a_pos, da) * a_unit + at(b_pos, db) * b_unit, at(zpos, dz) * 2 + core)

    twin = (grp, zpos * 2 + 1 - core)

    sizes = []

    def send(src, dst, to):
        n = len(sizes)
        sizes.append(src)
        pltpu.make_async_remote_copy(
            src_ref=src, dst_ref=dst, send_sem=send_sem.at[n], recv_sem=recv_sem.at[n],
            device_id=to, device_id_type=MESH,
        ).start()
        return n

    def arrive(n, ref):
        pltpu.make_async_remote_copy(
            src_ref=ref, dst_ref=ref, send_sem=send_sem.at[n], recv_sem=recv_sem.at[n],
            device_id=twin, device_id_type=MESH,
        ).wait_recv()

    def sent(n, ref):
        pltpu.make_async_remote_copy(
            src_ref=ref, dst_ref=ref, send_sem=send_sem.at[n], recv_sem=recv_sem.at[n],
            device_id=twin, device_id_type=MESH,
        ).wait_send()

    def shard(dz, c=None):
        return at(zpos, dz) * 2 + (core if c is None else c)

    def direct(dz, half=None, c=None):
        start = shard(dz, c) * OWN_LAGS
        if half is None:
            return table.at[pl.ds(start, 8)]
        return table.at[pl.ds(start + 4 * half, 4)]

    def one(dz, da):
        s = b_pos * SIDE + at(a_pos, da)
        return table.at[pl.ds((1 + s // 8) * LAGS + shard(dz) * OWN_LAGS + lax.rem(s, 8), 1)]

    def row(dz, db, half=None, bb=None, c=None):
        b = at(b_pos, db) if bb is None else bb
        start = (1 + b // 2) * LAGS + shard(dz, c) * OWN_LAGS + lax.rem(b, 2) * 4
        if half is None:
            return table.at[pl.ds(start, 4)]
        return table.at[pl.ds(start + 2 * half, 2)]

    loads = [
        pltpu.make_async_copy(
            w_hbm.at[pl.ds(k * OWN_LAGS, OWN_LAGS)],
            table.at[pl.ds(k * LAGS + lag * OWN_LAGS, OWN_LAGS)],
            load_sem.at[k],
        )
        for k in range(CLASSES)
    ]
    hist = [
        pltpu.make_async_copy(h_hbm.at[s], hist_in.at[s % 2], hist_sem.at[s]) for s in range(OWNED)
    ]
    hist[0].start()
    hist[1].start()

    barrier = pltpu.get_barrier_semaphore()
    partners = [twin]
    for d in (1, 2, 3):
        partners += [device(da=d), device(db=d), device(dz=d)]
    for p in partners:
        pl.semaphore_signal(barrier, inc=1, device_id=p, device_id_type=MESH)

    for b in range(SIDE):
        for a in range(SIDE):
            for s in range(SLOTS):
                value = recv_target[s, a * a_unit + b * b_unit]
                target_own[b, pl.ds(a * SLOTS + s, 1), :] = jnp.full((1, PANEL), value, jnp.int32)
    target_row[3] = target_own[b_pos]
    pl.semaphore_wait(barrier, len(partners))

    own = b_pos * SIDE + a_pos
    slice_id = {}
    for dz in (1, 3, 2):
        slice_id[dz] = send(w_hbm.at[pl.ds(8 + own, 1)], one(0, 0), device(dz=dz))
    direct_id = {}
    for first in (True, False):
        for dz in (1, 3):
            half = (0 if dz == 1 else 1) if first else (1 if dz == 1 else 0)
            direct_id[dz, half] = send(w_hbm.at[pl.ds(4 * half, 4)], direct(0, half), device(dz=dz))
    target_id = {}
    for dd in (1, 2, 3):
        target_id[3 - dd] = send(target_own.at[at(b_pos, dd)], target_row.at[3 - dd], device(db=dd))
    for copy in loads:
        copy.start()
    twin_in = []
    for k in range(CLASSES):
        n = send(
            w_hbm.at[pl.ds(k * OWN_LAGS, OWN_LAGS)],
            table.at[pl.ds(k * LAGS + lag * OWN_LAGS, OWN_LAGS)],
            twin,
        )
        twin_in.append((n, table.at[pl.ds(k * LAGS + shard(0, 1 - core) * OWN_LAGS, OWN_LAGS)]))

    def turn(s):
        hist[s].wait()

        @pl.loop(0, STEPS)
        def _(m):
            block = hist_in[s % 2, pl.ds(pl.multiple_of(m * PANEL, PANEL), PANEL), :]
            hist_t[s, :, pl.ds(pl.multiple_of(m * PANEL, PANEL), PANEL)] = block.T

    turn(0)
    hist[2].start()
    turn(1)
    hist[3].start()

    first_id = {}
    for dz in (1, 3, 2):
        arrive(slice_id[dz], one(-dz % 4, 0))
        for da in (1, 3, 2):
            first_id[dz, da] = send(one(-dz % 4, 0), one(-dz % 4, 0), device(da=da))
    turn(2)
    turn(3)
    zero = jnp.zeros((PANEL, PANEL), jnp.float32)
    for t in range(OWNED):
        near_ref[t] = zero

    second_id = {}
    for dz in (1, 3, 2):
        for da in (1, 3, 2):
            arrive(first_id[dz, da], one(-dz % 4, -da % 4))
        for db, half in ((1, 0), (3, 1), (1, 1), (3, 0)):
            second_id[dz, db, half] = send(row(-dz % 4, 0, half), row(-dz % 4, 0, half), device(db=db))
        n = send(row(-dz % 4, 0), row(-dz % 4, 0), twin)
        twin_in.append((n, row(-dz % 4, 0, bb=jnp.where(core == 0, xpos, ypos), c=1 - core)))

    relay_id = {}
    for dz, half in ((1, 0), (3, 1)):
        arrive(direct_id[dz, half], direct(-dz % 4, half))
        relay_id[dz] = send(direct(-dz % 4, half), direct(-dz % 4, half), device(dz=dz))
    for dz, half in ((1, 1), (3, 0)):
        arrive(direct_id[dz, half], direct(-dz % 4, half))
        n = send(direct(-dz % 4), direct(-dz % 4), twin)
        twin_in.append((n, direct(-dz % 4, c=1 - core)))

    pass_id = {}
    for dz in (1, 3, 2):
        for db, half in ((1, 0), (3, 1)):
            arrive(second_id[dz, db, half], row(-dz % 4, -db % 4, half))
            pass_id[dz, db] = send(row(-dz % 4, -db % 4, half), row(-dz % 4, -db % 4, half), device(db=db))
        for db, half in ((1, 1), (3, 0)):
            arrive(second_id[dz, db, half], row(-dz % 4, -db % 4, half))
            n = send(row(-dz % 4, -db % 4), row(-dz % 4, -db % 4), twin)
            other = at(a_pos, -db % 4)
            twin_in.append((n, row(-dz % 4, 0, bb=other, c=1 - core)))
    for dz, half in ((1, 0), (3, 1)):
        arrive(relay_id[dz], direct(2, half))
    n = send(direct(2), direct(2), twin)
    twin_in.append((n, direct(2, c=1 - core)))
    for dz in (1, 3, 2):
        for db, half in ((1, 0), (3, 1)):
            arrive(pass_id[dz, db], row(-dz % 4, 2, half))
        n = send(row(-dz % 4, 2), row(-dz % 4, 2), twin)
        twin_in.append((n, row(-dz % 4, 0, bb=at(a_pos, 2), c=1 - core)))
    for n, ref in twin_in:
        arrive(n, ref)
    for copy in loads:
        copy.wait()

    def product(klass, offset, patch):
        window = table[pl.ds(klass * LAGS + offset, STEPS)].reshape(STEPS * PANEL, PANEL)
        return jnp.dot(hist_t[patch], window, preferred_element_type=jnp.float32)

    def pair_copy(q):
        da = lax.rem(lax.rem(q, 4) + 1, 4)
        return pltpu.make_async_remote_copy(
            src_ref=send_buf.at[pl.ds(q * SLOTS, SLOTS)], dst_ref=recv_buf.at[pl.ds(q * SLOTS, SLOTS)],
            send_sem=pair_send.at[q], recv_sem=pair_recv.at[q],
            device_id=device(da=da), device_id_type=MESH,
        )

    @pl.loop(0, SIDE * SIDE)
    def _(q):
        db = q // 4
        da = lax.rem(lax.rem(q, 4) + 1, 4)
        peer = at(a_pos, da) * a_unit + at(b_pos, db + 1) * b_unit
        for s in range(SLOTS):
            block = product(send_class[s, peer], send_lag[s, peer], send_patch[s, peer])
            send_buf[q * SLOTS + s] = block.astype(jnp.bfloat16)

        @pl.when(da != 0)
        def _():
            pair_copy(q).start()

    def local(first, count):
        @pl.loop(first, first + count)
        def _(group):
            @pl.loop(0, GROUP)
            def _(i):
                j = group * GROUP + i
                contrib[i] = product(local_class[j], local_lag[j], local_src[j])

            @pl.loop(0, PANEL // 32)
            def _(chunk):
                rows = pl.ds(pl.multiple_of(chunk * 32, 32), 32)
                totals = [near_ref[t, rows, :] for t in range(OWNED)]
                for i in range(GROUP):
                    part = contrib[i, rows, :]
                    target = local_target[group * GROUP + i]
                    for t in range(OWNED):
                        totals[t] += jnp.where(target == t, part, 0.0)
                for t in range(OWNED):
                    near_ref[t, rows, :] = totals[t]

    def merge(db):
        for r in range(3):
            pair_copy(db * 4 + r).wait_recv()

        @pl.loop(0, PANEL // 16)
        def _(chunk):
            rows = pl.ds(pl.multiple_of(chunk * 16, 16), 16)
            totals = [None] * OWNED
            for r in range(4):
                da = (r + 1) % 4
                source = at(a_pos, -da % 4)
                buffer = send_buf if da == 0 else recv_buf
                for s in range(SLOTS):
                    part = buffer[(db * 4 + r) * SLOTS + s, rows, :].astype(jnp.float32)
                    which = target_row[db, pl.ds(source * SLOTS + s, 1), :]
                    for t in range(OWNED):
                        kept = jnp.where(jnp.broadcast_to(which, part.shape) == t, part, 0.0)
                        totals[t] = kept if totals[t] is None else totals[t] + kept
            for t in range(OWNED):
                if db < 3:
                    merged[db * OWNED + t, rows, :] = totals[t].astype(jnp.bfloat16)
                else:
                    near_ref[t, rows, :] += totals[t]

    def merged_copy(db):
        return pltpu.make_async_remote_copy(
            src_ref=merged.at[pl.ds(db * OWNED, OWNED)], dst_ref=arrived.at[pl.ds(db * OWNED, OWNED)],
            send_sem=pair_send.at[16 + db], recv_sem=pair_recv.at[16 + db],
            device_id=device(db=db + 1), device_id_type=MESH,
        )

    for db in range(3):
        arrive(target_id[db], target_row.at[db])
    for db in range(3):
        merge(db)
        merged_copy(db).start()
        local(2 * db, 2)
    merge(3)
    for db in range(3):
        merged_copy(db).wait_recv()

    @pl.loop(0, PANEL // 16)
    def _(chunk):
        rows = pl.ds(pl.multiple_of(chunk * 16, 16), 16)
        for t in range(OWNED):
            total = near_ref[t, rows, :]
            for db in range(3):
                total += arrived[db * OWNED + t, rows, :].astype(jnp.float32)
            near_ref[t, rows, :] = total

    for db in range(4):
        for r in range(3):
            pair_copy(db * 4 + r).wait_send()
    for db in range(3):
        merged_copy(db).wait_send()
    for n, ref in enumerate(sizes):
        sent(n, ref)


def near_field(weights, history, tables):
    vmem = pltpu.VMEM
    smem = pl.BlockSpec(memory_space=pltpu.SMEM)
    anywhere = pl.BlockSpec(memory_space=pl.ANY)
    return pl.pallas_call(
        near_kernel,
        out_shape=jax.ShapeDtypeStruct((OWNED, PANEL, PANEL), jnp.float32),
        in_specs=[anywhere, anywhere] + [smem] * 8,
        out_specs=pl.BlockSpec(memory_space=vmem),
        scratch_shapes=[
            vmem((CLASSES * LAGS, PANEL, PANEL), jnp.bfloat16),
            vmem((OWNED, PANEL, STEPS * PANEL), jnp.bfloat16),
            vmem((2, STEPS * PANEL, PANEL), jnp.bfloat16),
            vmem((32, PANEL, PANEL), jnp.bfloat16),
            vmem((32, PANEL, PANEL), jnp.bfloat16),
            vmem((12, PANEL, PANEL), jnp.bfloat16),
            vmem((12, PANEL, PANEL), jnp.bfloat16),
            vmem((GROUP, PANEL, PANEL), jnp.float32),
            vmem((SIDE, SIDE * SLOTS, PANEL), jnp.int32),
            vmem((SIDE, SIDE * SLOTS, PANEL), jnp.int32),
            pltpu.SemaphoreType.DMA((80,)),
            pltpu.SemaphoreType.DMA((80,)),
            pltpu.SemaphoreType.DMA((19,)),
            pltpu.SemaphoreType.DMA((19,)),
            pltpu.SemaphoreType.DMA((CLASSES,)),
            pltpu.SemaphoreType.DMA((OWNED,)),
        ],
        compiler_params=pltpu.CompilerParams(
            collective_id=0, has_side_effects=True, vmem_limit_bytes=60 * 2**20
        ),
    )(weights.reshape(CLASSES * OWN_LAGS, PANEL, PANEL), history, *tables)


def per_device(
    weights, history, send_patch, send_lag, send_class, recv_target,
    local_src, local_lag, local_class, local_target, inverse_blocks, incident,
):
    near_t = near_field(
        weights, history,
        (send_patch.T, send_lag.T, send_class.T, recv_target.T, local_src, local_lag, local_class, local_target),
    )
    near_sum = jnp.swapaxes(near_t, 1, 2)
    residual = (incident.astype(jnp.float32) - near_sum).astype(jnp.bfloat16)
    density = jnp.einsum("tpq,tqc->tpc", inverse_blocks, residual, preferred_element_type=jnp.float32)
    return density.astype(jnp.bfloat16)


def solution(mesh):
    both = ("grp", "lag")
    return jax.shard_map(
        per_device,
        mesh=mesh,
        in_specs=(
            P(None, "lag", None), P(both, None, None),
            P(both, None), P(both, None), P(both, None), P(both, None),
            P(both), P(both), P(both), P(both),
            P(both, None, None), P(both, None, None),
        ),
        out_specs=P(both, None, None),
        check_vma=False,
    )
```

```python
import jax
import jax.numpy as jnp
from jax import lax
from jax.experimental import pallas as pl
from jax.experimental.pallas import tpu as pltpu
from jax.sharding import PartitionSpec as P

MESH = pl.DeviceIdType.MESH
PANEL = 256
STEPS = 8
LAGS = 64
OWN_LAGS = 8
CLASSES = 3
OWNED = 4
SIDE = 4
SLOTS = 2
NLOC = 48
GROUP = 8
HALF = 128
SHARD = 2048
PIECE_ROWS = (32, 16)
CHUNKS = (4, 2)
NCOPY = 112


def near_kernel(
    w_hbm, h_hbm, inverse_hbm, incident_hbm, send_patch, send_lag, send_class, recv_target,
    local_src, local_lag, local_class, local_target,
    out_ref,
    table0, table1, hist, shard_in, inverse, incident, near, send_buf, recv_buf, merged, arrived, contrib,
    target_own, target_row,
    send_sem, recv_sem, pair_send, pair_recv, load_sem,
):
    tables = (table0, table1)
    grp = lax.axis_index("grp")
    lag = lax.axis_index("lag")
    core = lax.rem(lag, 2)
    zpos = lag // 2
    xpos = lax.rem(grp, SIDE)
    ypos = grp // SIDE
    a_pos = jnp.where(core == 0, xpos, ypos)
    b_pos = jnp.where(core == 0, ypos, xpos)
    a_unit = jnp.where(core == 0, 1, SIDE)
    b_unit = jnp.where(core == 0, SIDE, 1)

    def at(pos, step):
        return lax.rem(pos + step % SIDE, SIDE)

    def device(da=0, db=0, dz=0):
        return (at(a_pos, da) * a_unit + at(b_pos, db) * b_unit, at(zpos, dz) * 2 + core)

    twin = (grp, zpos * 2 + 1 - core)

    copies = []

    def remote(n, src, dst, to):
        return pltpu.make_async_remote_copy(
            src_ref=src, dst_ref=dst, send_sem=send_sem.at[n], recv_sem=recv_sem.at[n],
            device_id=to, device_id_type=MESH,
        )

    def send(ref, to):
        n = len(copies)
        copies.append(ref)
        remote(n, ref, ref, to).start()
        return n

    def arrive(n, ref):
        remote(n, ref, ref, twin).wait_recv()

    def shard(dz, c=None):
        return at(zpos, dz) * 2 + (core if c is None else c)

    def piece(x, l, b, chunk=None):
        rows = PIECE_ROWS[x]
        count = OWN_LAGS if chunk is None else OWN_LAGS // CHUNKS[x]
        start = l * OWN_LAGS + (0 if chunk is None else chunk * count)
        return tables[x].at[:, pl.ds(start, count), pl.ds(pl.multiple_of(b * rows, rows), rows)]

    def deep(l, half=None):
        count = OWN_LAGS if half is None else OWN_LAGS // 2
        start = l * OWN_LAGS + (0 if half is None else half * count)
        return table1.at[:, pl.ds(start, count), pl.ds(HALF // 2, HALF // 2)]

    def whole(x, l):
        return tables[x].at[:, pl.ds(l * OWN_LAGS, OWN_LAGS)]

    shard_loads = [
        pltpu.make_async_copy(
            w_hbm.at[:, pl.ds(c * 512, 512)], shard_in.at[:, pl.ds(c * 512, 512)], load_sem.at[4 + c]
        )
        for c in range(4)
    ]
    hist_load = pltpu.make_async_copy(h_hbm, hist, load_sem.at[1])
    inverse_load = pltpu.make_async_copy(inverse_hbm, inverse, load_sem.at[2])
    incident_load = pltpu.make_async_copy(incident_hbm, incident, load_sem.at[3])
    for c in (0, 3, 1, 2):
        shard_loads[c].start()

    barrier = pltpu.get_barrier_semaphore()
    partners = [twin]
    for d in (1, 2, 3):
        partners += [device(da=d), device(db=d), device(dz=d)]
    for p in partners:
        pl.semaphore_signal(barrier, inc=1, device_id=p, device_id_type=MESH)

    for b in range(SIDE):
        for a in range(SIDE):
            for s in range(SLOTS):
                value = recv_target[s, a * a_unit + b * b_unit]
                target_own[b, pl.ds(a * SLOTS + s, 1), :] = jnp.full((1, PANEL), value, jnp.int32)
    target_row[3] = target_own[b_pos]

    def turn(x, c):
        @pl.loop(0, 2 * CLASSES)
        def _(n):
            i = 2 * c + lax.rem(n, 2)
            rows = pl.ds(pl.multiple_of(i * PANEL, PANEL), PANEL)
            tables[x][n // 2, lag * OWN_LAGS + i] = shard_in[n // 2, rows, pl.ds(x * HALF, HALF)].T

    z_id, relay_id, b_id, pass_id, deep_id, target_id = {}, {}, {}, {}, {}, {}
    twin_in = ([], [])

    def to_twin(x, ref, there):
        twin_in[x].append((send(ref, twin), there))

    def passed_on(x, step, chunk):
        return chunk < CHUNKS[x] // 2 if step == 1 else chunk >= CHUNKS[x] // 2

    def order(x, step):
        n = CHUNKS[x]
        if step == 1:
            return list(range(n))
        if step == 3:
            return list(range(n))[::-1]
        return [c for i in range(n // 2) for c in (i, n - 1 - i)]

    def z_send(x):
        for pair in zip(order(x, 1), order(x, 3)):
            for dz, c in zip((1, 3), pair):
                z_id[x, dz, c] = send(piece(x, lag, b_pos, c), device(dz=dz))

    def b_send(x, dz, c):
        for db in (1, 3):
            b_id[x, dz, db, c] = send(piece(x, shard(dz), b_pos, c), device(db=db))

    def z_recv(x):
        for pair in zip(order(x, 1), order(x, 3)):
            for dz, c in zip((1, 3), pair):
                ref = piece(x, shard(-dz), b_pos, c)
                arrive(z_id[x, dz, c], ref)
                if passed_on(x, dz, c):
                    relay_id[x, c] = send(ref, device(dz=dz))
                b_send(x, -dz % 4, c)

    def z_relay_recv(x):
        for c in order(x, 2):
            arrive(relay_id[x, c], piece(x, shard(2), b_pos, c))
            b_send(x, 2, c)

    def b_recv(x, dz):
        for c in order(x, -dz % 4):
            for db in (1, 3):
                ref = piece(x, shard(dz), at(b_pos, -db), c)
                arrive(b_id[x, dz, db, c], ref)
                if passed_on(x, db, c):
                    pass_id[x, dz, c] = send(ref, device(db=db))
        for db in (0, 1, 3):
            to_twin(x, piece(x, shard(dz), at(b_pos, db)), piece(x, shard(dz, 1 - core), at(a_pos, db)))

    def b_pass_recv(x, dz):
        for c in order(x, -dz % 4):
            arrive(pass_id[x, dz, c], piece(x, shard(dz), at(b_pos, 2), c))
        to_twin(x, piece(x, shard(dz), at(b_pos, 2)), piece(x, shard(dz, 1 - core), at(a_pos, 2)))

    def deep_send():
        for step in (0, 1):
            for dz, half in ((1, step), (3, 1 - step)):
                deep_id[dz, half] = send(deep(lag, half), device(dz=dz))

    def deep_relay():
        for dz, half in ((1, 0), (3, 1)):
            arrive(deep_id[dz, half], deep(shard(-dz), half))
            deep_id[2, half] = send(deep(shard(-dz), half), device(dz=dz))

    def deep_rest():
        for dz, half in ((1, 1), (3, 0)):
            arrive(deep_id[dz, half], deep(shard(-dz), half))
            to_twin(1, deep(shard(-dz)), deep(shard(-dz, 1 - core)))

    def deep_last():
        for half in (0, 1):
            arrive(deep_id[2, half], deep(shard(2), half))
        to_twin(1, deep(shard(2)), deep(shard(2, 1 - core)))

    def table_done(x):
        for n, ref in twin_in[x]:
            arrive(n, ref)

    def product(x, klass, offset, patch):
        blocks = tables[x][klass, pl.ds(offset, STEPS)]
        window = jnp.concatenate([blocks[m] for m in range(STEPS)], axis=1)
        return jnp.dot(window, hist[patch], preferred_element_type=jnp.float32)

    def pair_copy(x, q):
        da = lax.rem(lax.rem(q, 4) + 1, 4)
        blocks = pl.ds(q * SLOTS, SLOTS)
        return pltpu.make_async_remote_copy(
            src_ref=send_buf.at[x, blocks], dst_ref=recv_buf.at[x, blocks],
            send_sem=pair_send.at[x, q], recv_sem=pair_recv.at[x, q],
            device_id=device(da=da), device_id_type=MESH,
        )

    def served(x):
        @pl.loop(0, SIDE * SIDE // 2)
        def _(step):
            for q in (step * 2, step * 2 + 1):
                da = lax.rem(lax.rem(q, 4) + 1, 4)
                peer = lax.rem(a_pos + da, SIDE) * a_unit + lax.rem(b_pos + q // 4 + 1, SIDE) * b_unit
                for s in range(SLOTS):
                    block = product(x, send_class[s, peer], send_lag[s, peer], send_patch[s, peer])
                    send_buf[x, q * SLOTS + s] = block.astype(jnp.bfloat16)
            pair_copy(x, step * 2).start()

            @pl.when(lax.rem(step, 2) == 0)
            def _():
                pair_copy(x, step * 2 + 1).start()

    def local(x, first, count):
        @pl.loop(first, first + count)
        def _(group):
            @pl.loop(0, GROUP // 4)
            def _(i):
                for s in range(4):
                    j = group * GROUP + i * 4 + s
                    contrib[i * 4 + s] = product(x, local_class[j], local_lag[j], local_src[j])

            @pl.loop(0, HALF // 32)
            def _(chunk):
                rows = pl.ds(pl.multiple_of(chunk * 32, 32), 32)
                totals = [near[x, t, rows, :] for t in range(OWNED)]
                for i in range(GROUP):
                    part = contrib[i, rows, :]
                    target = local_target[group * GROUP + i]
                    for t in range(OWNED):
                        totals[t] += jnp.where(target == t, part, 0.0)
                for t in range(OWNED):
                    near[x, t, rows, :] = totals[t]

    def merge(x, db):
        for r in range(3):
            pair_copy(x, db * 4 + r).wait_recv()

        @pl.loop(0, HALF // 16)
        def _(chunk):
            rows = pl.ds(pl.multiple_of(chunk * 16, 16), 16)
            totals = [None] * OWNED
            for r in range(4):
                da = (r + 1) % 4
                source = at(a_pos, -da)
                buffer = send_buf if da == 0 else recv_buf
                for s in range(SLOTS):
                    part = buffer[x, (db * 4 + r) * SLOTS + s, rows, :].astype(jnp.float32)
                    which = target_row[db, pl.ds(source * SLOTS + s, 1), :]
                    for t in range(OWNED):
                        kept = jnp.where(jnp.broadcast_to(which, part.shape) == t, part, 0.0)
                        totals[t] = kept if totals[t] is None else totals[t] + kept
            for t in range(OWNED):
                if db < 3:
                    merged[x, db * OWNED + t, rows, :] = totals[t].astype(jnp.bfloat16)
                else:
                    near[x, t, rows, :] += totals[t]

        if db < 3:
            merged_copy(x, db).start()

    def merged_copy(x, db):
        blocks = pl.ds(db * OWNED, OWNED)
        return pltpu.make_async_remote_copy(
            src_ref=merged.at[x, blocks], dst_ref=arrived.at[x, blocks],
            send_sem=pair_send.at[x, 16 + db], recv_sem=pair_recv.at[x, 16 + db],
            device_id=device(db=db + 1), device_id_type=MESH,
        )

    def z_one(x, dz, c):
        z_id[x, dz, c] = send(piece(x, lag, b_pos, c), device(dz=dz))

    pl.semaphore_wait(barrier, len(partners))
    for dz, c in ((1, 0), (3, 3), (1, 1), (3, 2)):
        shard_loads[c].wait()
        turn(0, c)
        z_one(0, dz, c)
    for dz, c in ((1, 2), (3, 1), (1, 3), (3, 0)):
        z_one(0, dz, c)
    for c in range(4):
        turn(1, c)
    for x in (0, 1):
        to_twin(x, whole(x, lag), whole(x, shard(0, 1 - core)))
    for dd in (1, 2, 3):
        n = len(copies)
        copies.append(target_own.at[at(b_pos, dd)])
        remote(n, target_own.at[at(b_pos, dd)], target_row.at[3 - dd], device(db=dd)).start()
        target_id[3 - dd] = n
    hist_load.start()
    inverse_load.start()
    incident_load.start()
    zero = jnp.zeros((HALF, PANEL), jnp.float32)
    for x in (0, 1):
        for t in range(OWNED):
            near[x, t] = zero

    z_recv(0)
    z_send(1)
    deep_send()
    b_recv(0, 3)
    b_recv(0, 1)
    z_relay_recv(0)
    b_recv(0, 2)
    z_recv(1)
    for dz in (3, 1, 2):
        b_pass_recv(0, dz)
    hist_load.wait()
    for db in range(3):
        arrive(target_id[db], target_row.at[db])
    table_done(0)

    served(0)
    z_relay_recv(1)
    deep_relay()
    b_recv(1, 3)
    b_recv(1, 1)
    local(0, 0, 2)
    b_recv(1, 2)
    merge(0, 0)
    local(0, 2, 1)
    merge(0, 1)
    for dz in (3, 1, 2):
        b_pass_recv(1, dz)
    deep_rest()
    local(0, 3, 1)
    merge(0, 2)
    deep_last()
    local(0, 4, 1)
    table_done(1)

    served(1)
    merge(0, 3)
    local(0, 5, 1)
    for db in range(3):
        merge(1, db)
        local(1, 2 * db, 2)
    merge(1, 3)
    inverse_load.wait()
    incident_load.wait()
    for x in (0, 1):
        for db in range(3):
            merged_copy(x, db).wait_recv()
    @pl.loop(0, HALF // 16)
    def _(chunk):
        rows = pl.ds(pl.multiple_of(chunk * 16, 16), 16)
        for x in (0, 1):
            whole_rows = pl.ds(pl.multiple_of(x * HALF + chunk * 16, 16), 16)
            for t in range(OWNED):
                total = near[x, t, rows, :]
                for db in range(3):
                    total += arrived[x, db * OWNED + t, rows, :].astype(jnp.float32)
                residual = incident[t, whole_rows, :].astype(jnp.float32) - total
                incident[t, whole_rows, :] = residual.astype(jnp.bfloat16)

    for t in range(OWNED):
        density = jnp.dot(inverse[t], incident[t], preferred_element_type=jnp.float32)
        out_ref[t] = density.astype(jnp.bfloat16)

    for x in (0, 1):
        for db in range(4):
            for r in range(3):
                pair_copy(x, db * 4 + r).wait_send()
        for db in range(3):
            merged_copy(x, db).wait_send()
    for n, ref in enumerate(copies):
        remote(n, ref, ref, twin).wait_send()


def near_field(weights, history, inverse_blocks, incident, tables):
    vmem = pltpu.VMEM
    dma = pltpu.SemaphoreType.DMA
    smem = pl.BlockSpec(memory_space=pltpu.SMEM)
    anywhere = pl.BlockSpec(memory_space=pl.ANY)
    half = jnp.bfloat16
    return pl.pallas_call(
        near_kernel,
        out_shape=jax.ShapeDtypeStruct((OWNED, PANEL, PANEL), half),
        in_specs=[anywhere] * 4 + [smem] * 8,
        out_specs=pl.BlockSpec(memory_space=vmem),
        scratch_shapes=[
            vmem((CLASSES, LAGS, HALF, PANEL), half),
            vmem((CLASSES, LAGS, HALF, PANEL), half),
            vmem((OWNED, STEPS * PANEL, PANEL), half),
            vmem((CLASSES, SHARD, PANEL), half),
            vmem((OWNED, PANEL, PANEL), half),
            vmem((OWNED, PANEL, PANEL), half),
            vmem((2, OWNED, HALF, PANEL), jnp.float32),
            vmem((2, 32, HALF, PANEL), half),
            vmem((2, 32, HALF, PANEL), half),
            vmem((2, 12, HALF, PANEL), half),
            vmem((2, 12, HALF, PANEL), half),
            vmem((GROUP, HALF, PANEL), jnp.float32),
            vmem((SIDE, SIDE * SLOTS, PANEL), jnp.int32),
            vmem((SIDE, SIDE * SLOTS, PANEL), jnp.int32),
            dma((NCOPY,)),
            dma((NCOPY,)),
            dma((2, 19)),
            dma((2, 19)),
            dma((8,)),
        ],
        compiler_params=pltpu.CompilerParams(
            collective_id=0, has_side_effects=True, vmem_limit_bytes=60 * 2**20
        ),
    )(weights, history, inverse_blocks, incident, *tables)


def per_device(
    weights, history, send_patch, send_lag, send_class, recv_target,
    local_src, local_lag, local_class, local_target, inverse_blocks, incident,
):
    return near_field(
        weights, history, inverse_blocks, incident,
        (send_patch.T, send_lag.T, send_class.T, recv_target.T, local_src, local_lag, local_class, local_target),
    )


def solution(mesh):
    both = ("grp", "lag")
    return jax.shard_map(
        per_device,
        mesh=mesh,
        in_specs=(
            P(None, "lag", None), P(both, None, None),
            P(both, None), P(both, None), P(both, None), P(both, None),
            P(both), P(both), P(both), P(both),
            P(both, None, None), P(both, None, None),
        ),
        out_specs=P(both, None, None),
        check_vma=False,
    )
```

```python
import jax
import jax.numpy as jnp
from jax import lax
from jax.experimental import pallas as pl
from jax.experimental.pallas import tpu as pltpu
from jax.sharding import PartitionSpec as P

MESH = pl.DeviceIdType.MESH
PANEL = 256
STEPS = 8
LAGS = 64
OWN_LAGS = 8
CLASSES = 3
OWNED = 4
SIDE = 4
SLOTS = 2
NLOC = 48
GROUP = 8
HALF = 128
SHARD = 2048
PIECE_ROWS = (32, 16)
CHUNKS = (4, 2)
NCOPY = 112


def near_kernel(
    w_hbm, h_hbm, inverse_hbm, incident_hbm, send_patch, send_lag, send_class, recv_target,
    local_src, local_lag, local_class, local_target,
    out_ref,
    table0, table1, hist, shard_in, inverse, incident, near, send_buf, recv_buf, merged, arrived, contrib,
    target_own, target_row,
    send_sem, recv_sem, pair_send, pair_recv, load_sem,
):
    tables = (table0, table1)
    grp = lax.axis_index("grp")
    lag = lax.axis_index("lag")
    core = lax.rem(lag, 2)
    zpos = lag // 2
    xpos = lax.rem(grp, SIDE)
    ypos = grp // SIDE
    a_pos = jnp.where(core == 0, xpos, ypos)
    b_pos = jnp.where(core == 0, ypos, xpos)
    a_unit = jnp.where(core == 0, 1, SIDE)
    b_unit = jnp.where(core == 0, SIDE, 1)

    def at(pos, step):
        return lax.rem(pos + step % SIDE, SIDE)

    def device(da=0, db=0, dz=0):
        return (at(a_pos, da) * a_unit + at(b_pos, db) * b_unit, at(zpos, dz) * 2 + core)

    twin = (grp, zpos * 2 + 1 - core)

    copies = []

    def remote(n, src, dst, to):
        return pltpu.make_async_remote_copy(
            src_ref=src, dst_ref=dst, send_sem=send_sem.at[n], recv_sem=recv_sem.at[n],
            device_id=to, device_id_type=MESH,
        )

    def send(ref, to):
        n = len(copies)
        copies.append(ref)
        remote(n, ref, ref, to).start()
        return n

    def arrive(n, ref):
        remote(n, ref, ref, twin).wait_recv()

    def shard(dz, c=None):
        return at(zpos, dz) * 2 + (core if c is None else c)

    def piece(x, l, b, chunk=None):
        rows = PIECE_ROWS[x]
        count = OWN_LAGS if chunk is None else OWN_LAGS // CHUNKS[x]
        start = l * OWN_LAGS + (0 if chunk is None else chunk * count)
        return tables[x].at[:, pl.ds(start, count), pl.ds(pl.multiple_of(b * rows, rows), rows)]

    def deep(l, half=None):
        count = OWN_LAGS if half is None else OWN_LAGS // 2
        start = l * OWN_LAGS + (0 if half is None else half * count)
        return table1.at[:, pl.ds(start, count), pl.ds(HALF // 2, HALF // 2)]

    def whole(x, l):
        return tables[x].at[:, pl.ds(l * OWN_LAGS, OWN_LAGS)]

    shard_loads = [
        pltpu.make_async_copy(
            w_hbm.at[:, pl.ds(c * 512, 512)], shard_in.at[:, pl.ds(c * 512, 512)], load_sem.at[4 + c]
        )
        for c in range(4)
    ]
    hist_load = pltpu.make_async_copy(h_hbm, hist, load_sem.at[1])
    inverse_load = pltpu.make_async_copy(inverse_hbm, inverse, load_sem.at[2])
    incident_load = pltpu.make_async_copy(incident_hbm, incident, load_sem.at[3])
    for c in (0, 3, 1, 2):
        shard_loads[c].start()

    barrier = pltpu.get_barrier_semaphore()
    partners = [twin]
    for d in (1, 2, 3):
        partners += [device(da=d), device(db=d), device(dz=d)]
    for p in partners:
        pl.semaphore_signal(barrier, inc=1, device_id=p, device_id_type=MESH)

    def turn(x, c):
        @pl.loop(0, 2 * CLASSES)
        def _(n):
            i = 2 * c + lax.rem(n, 2)
            rows = pl.ds(pl.multiple_of(i * PANEL, PANEL), PANEL)
            tables[x][n // 2, lag * OWN_LAGS + i] = shard_in[n // 2, rows, pl.ds(x * HALF, HALF)].T

    z_id, relay_id, b_id, pass_id, deep_id, target_id = {}, {}, {}, {}, {}, {}
    twin_in = ([], [])

    def to_twin(x, ref, there):
        twin_in[x].append((send(ref, twin), there))

    def passed_on(x, step, chunk):
        return chunk < CHUNKS[x] // 2 if step == 1 else chunk >= CHUNKS[x] // 2

    def order(x, step):
        n = CHUNKS[x]
        if step == 1:
            return list(range(n))
        if step == 3:
            return list(range(n))[::-1]
        return [c for i in range(n // 2) for c in (i, n - 1 - i)]

    def z_send(x):
        for pair in zip(order(x, 1), order(x, 3)):
            for dz, c in zip((1, 3), pair):
                z_id[x, dz, c] = send(piece(x, lag, b_pos, c), device(dz=dz))

    def b_send(x, dz, c):
        for db in (1, 3):
            b_id[x, dz, db, c] = send(piece(x, shard(dz), b_pos, c), device(db=db))

    def z_recv(x):
        for pair in zip(order(x, 1), order(x, 3)):
            for dz, c in zip((1, 3), pair):
                ref = piece(x, shard(-dz), b_pos, c)
                arrive(z_id[x, dz, c], ref)
                if passed_on(x, dz, c):
                    relay_id[x, c] = send(ref, device(dz=dz))
                b_send(x, -dz % 4, c)

    def z_relay_recv(x):
        for c in order(x, 2):
            arrive(relay_id[x, c], piece(x, shard(2), b_pos, c))
            b_send(x, 2, c)

    def b_recv(x, dz):
        for c in order(x, -dz % 4):
            for db in (1, 3):
                ref = piece(x, shard(dz), at(b_pos, -db), c)
                arrive(b_id[x, dz, db, c], ref)
                if passed_on(x, db, c):
                    pass_id[x, dz, c] = send(ref, device(db=db))
        for db in (0, 1, 3):
            to_twin(x, piece(x, shard(dz), at(b_pos, db)), piece(x, shard(dz, 1 - core), at(a_pos, db)))

    def b_pass_recv(x, dz):
        for c in order(x, -dz % 4):
            arrive(pass_id[x, dz, c], piece(x, shard(dz), at(b_pos, 2), c))
        to_twin(x, piece(x, shard(dz), at(b_pos, 2)), piece(x, shard(dz, 1 - core), at(a_pos, 2)))

    def deep_send():
        for step in (0, 1):
            for dz, half in ((1, step), (3, 1 - step)):
                deep_id[dz, half] = send(deep(lag, half), device(dz=dz))

    def deep_relay():
        for dz, half in ((1, 0), (3, 1)):
            arrive(deep_id[dz, half], deep(shard(-dz), half))
            deep_id[2, half] = send(deep(shard(-dz), half), device(dz=dz))

    def deep_rest():
        for dz, half in ((1, 1), (3, 0)):
            arrive(deep_id[dz, half], deep(shard(-dz), half))
            to_twin(1, deep(shard(-dz)), deep(shard(-dz, 1 - core)))

    def deep_last():
        for half in (0, 1):
            arrive(deep_id[2, half], deep(shard(2), half))
        to_twin(1, deep(shard(2)), deep(shard(2, 1 - core)))

    def table_done(x):
        for n, ref in twin_in[x]:
            arrive(n, ref)

    def product(x, klass, offset, patch):
        blocks = tables[x][klass, pl.ds(offset, STEPS)]
        window = jnp.concatenate([blocks[m] for m in range(STEPS)], axis=1)
        return jnp.dot(window, hist[patch], preferred_element_type=jnp.float32)

    def pair_copy(x, q):
        da = lax.rem(lax.rem(q, 4) + 1, 4)
        blocks = pl.ds(q * SLOTS, SLOTS)
        return pltpu.make_async_remote_copy(
            src_ref=send_buf.at[x, blocks], dst_ref=recv_buf.at[x, blocks],
            send_sem=pair_send.at[x, q], recv_sem=pair_recv.at[x, q],
            device_id=device(da=da), device_id_type=MESH,
        )

    def served(x):
        @pl.loop(0, SIDE * SIDE // 2)
        def _(step):
            for q in (step * 2, step * 2 + 1):
                da = lax.rem(lax.rem(q, 4) + 1, 4)
                peer = lax.rem(a_pos + da, SIDE) * a_unit + lax.rem(b_pos + q // 4 + 1, SIDE) * b_unit
                for s in range(SLOTS):
                    block = product(x, send_class[s, peer], send_lag[s, peer], send_patch[s, peer])
                    send_buf[x, q * SLOTS + s] = block.astype(jnp.bfloat16)
            pair_copy(x, step * 2).start()

            @pl.when(lax.rem(step, 2) == 0)
            def _():
                pair_copy(x, step * 2 + 1).start()

    def local(x, first, count):
        @pl.loop(first, first + count)
        def _(group):
            @pl.loop(0, GROUP // 4)
            def _(i):
                for s in range(4):
                    j = group * GROUP + i * 4 + s
                    contrib[i * 4 + s] = product(x, local_class[j], local_lag[j], local_src[j])

            @pl.loop(0, HALF // 32)
            def _(chunk):
                rows = pl.ds(pl.multiple_of(chunk * 32, 32), 32)
                totals = [near[x, t, rows, :] for t in range(OWNED)]
                for i in range(GROUP):
                    part = contrib[i, rows, :]
                    target = local_target[group * GROUP + i]
                    for t in range(OWNED):
                        totals[t] += jnp.where(target == t, part, 0.0)
                for t in range(OWNED):
                    near[x, t, rows, :] = totals[t]

    def merge(x, db):
        for r in range(3):
            pair_copy(x, db * 4 + r).wait_recv()

        @pl.loop(0, HALF // 16)
        def _(chunk):
            rows = pl.ds(pl.multiple_of(chunk * 16, 16), 16)
            totals = [None] * OWNED
            for r in range(4):
                da = (r + 1) % 4
                source = at(a_pos, -da)
                buffer = send_buf if da == 0 else recv_buf
                for s in range(SLOTS):
                    part = buffer[x, (db * 4 + r) * SLOTS + s, rows, :].astype(jnp.float32)
                    which = target_row[db, pl.ds(source * SLOTS + s, 1), :]
                    for t in range(OWNED):
                        kept = jnp.where(jnp.broadcast_to(which, part.shape) == t, part, 0.0)
                        totals[t] = kept if totals[t] is None else totals[t] + kept
            for t in range(OWNED):
                if db < 3:
                    merged[x, db * OWNED + t, rows, :] = totals[t].astype(jnp.bfloat16)
                else:
                    near[x, t, rows, :] += totals[t]

        if db < 3:
            merged_copy(x, db).start()

    def merged_copy(x, db):
        blocks = pl.ds(db * OWNED, OWNED)
        return pltpu.make_async_remote_copy(
            src_ref=merged.at[x, blocks], dst_ref=arrived.at[x, blocks],
            send_sem=pair_send.at[x, 16 + db], recv_sem=pair_recv.at[x, 16 + db],
            device_id=device(db=db + 1), device_id_type=MESH,
        )

    def z_one(x, dz, c):
        z_id[x, dz, c] = send(piece(x, lag, b_pos, c), device(dz=dz))

    pl.semaphore_wait(barrier, len(partners))
    for dz, c in ((1, 0), (3, 3), (1, 1), (3, 2)):
        shard_loads[c].wait()
        turn(0, c)
        z_one(0, dz, c)
    for dz, c in ((1, 2), (3, 1), (1, 3), (3, 0)):
        z_one(0, dz, c)
    for b in range(SIDE):
        for a in range(SIDE):
            for s in range(SLOTS):
                value = recv_target[s, a * a_unit + b * b_unit]
                target_own[b, pl.ds(a * SLOTS + s, 1), :] = jnp.full((1, PANEL), value, jnp.int32)
    target_row[3] = target_own[b_pos]

    for c in range(4):
        turn(1, c)
    for x in (0, 1):
        to_twin(x, whole(x, lag), whole(x, shard(0, 1 - core)))
    for dd in (1, 2, 3):
        n = len(copies)
        copies.append(target_own.at[at(b_pos, dd)])
        remote(n, target_own.at[at(b_pos, dd)], target_row.at[3 - dd], device(db=dd)).start()
        target_id[3 - dd] = n
    hist_load.start()
    inverse_load.start()
    incident_load.start()
    zero = jnp.zeros((HALF, PANEL), jnp.float32)
    for x in (0, 1):
        for t in range(OWNED):
            near[x, t] = zero

    z_recv(0)
    z_send(1)
    deep_send()
    b_recv(0, 3)
    b_recv(0, 1)
    z_relay_recv(0)
    b_recv(0, 2)
    z_recv(1)
    for dz in (3, 1, 2):
        b_pass_recv(0, dz)
    hist_load.wait()
    for db in range(3):
        arrive(target_id[db], target_row.at[db])
    table_done(0)

    served(0)
    z_relay_recv(1)
    deep_relay()
    b_recv(1, 3)
    b_recv(1, 1)
    local(0, 0, 2)
    b_recv(1, 2)
    merge(0, 0)
    local(0, 2, 1)
    merge(0, 1)
    for dz in (3, 1, 2):
        b_pass_recv(1, dz)
    deep_rest()
    local(0, 3, 1)
    merge(0, 2)
    deep_last()
    local(0, 4, 1)
    table_done(1)

    served(1)
    merge(0, 3)
    local(0, 5, 1)
    for db in range(3):
        merge(1, db)
        local(1, 2 * db, 2)
    merge(1, 3)
    inverse_load.wait()
    incident_load.wait()
    for x in (0, 1):
        for db in range(3):
            merged_copy(x, db).wait_recv()
    @pl.loop(0, HALF // 16)
    def _(chunk):
        rows = pl.ds(pl.multiple_of(chunk * 16, 16), 16)
        for x in (0, 1):
            whole_rows = pl.ds(pl.multiple_of(x * HALF + chunk * 16, 16), 16)
            for t in range(OWNED):
                total = near[x, t, rows, :]
                for db in range(3):
                    total += arrived[x, db * OWNED + t, rows, :].astype(jnp.float32)
                residual = incident[t, whole_rows, :].astype(jnp.float32) - total
                incident[t, whole_rows, :] = residual.astype(jnp.bfloat16)

    for t in range(OWNED):
        density = jnp.dot(inverse[t], incident[t], preferred_element_type=jnp.float32)
        out_ref[t] = density.astype(jnp.bfloat16)

    for x in (0, 1):
        for db in range(4):
            for r in range(3):
                pair_copy(x, db * 4 + r).wait_send()
        for db in range(3):
            merged_copy(x, db).wait_send()
    for n, ref in enumerate(copies):
        remote(n, ref, ref, twin).wait_send()


def near_field(weights, history, inverse_blocks, incident, tables):
    vmem = pltpu.VMEM
    dma = pltpu.SemaphoreType.DMA
    smem = pl.BlockSpec(memory_space=pltpu.SMEM)
    anywhere = pl.BlockSpec(memory_space=pl.ANY)
    half = jnp.bfloat16
    return pl.pallas_call(
        near_kernel,
        out_shape=jax.ShapeDtypeStruct((OWNED, PANEL, PANEL), half),
        in_specs=[anywhere] * 4 + [smem] * 8,
        out_specs=pl.BlockSpec(memory_space=vmem),
        scratch_shapes=[
            vmem((CLASSES, LAGS, HALF, PANEL), half),
            vmem((CLASSES, LAGS, HALF, PANEL), half),
            vmem((OWNED, STEPS * PANEL, PANEL), half),
            vmem((CLASSES, SHARD, PANEL), half),
            vmem((OWNED, PANEL, PANEL), half),
            vmem((OWNED, PANEL, PANEL), half),
            vmem((2, OWNED, HALF, PANEL), jnp.float32),
            vmem((2, 32, HALF, PANEL), half),
            vmem((2, 32, HALF, PANEL), half),
            vmem((2, 12, HALF, PANEL), half),
            vmem((2, 12, HALF, PANEL), half),
            vmem((GROUP, HALF, PANEL), jnp.float32),
            vmem((SIDE, SIDE * SLOTS, PANEL), jnp.int32),
            vmem((SIDE, SIDE * SLOTS, PANEL), jnp.int32),
            dma((NCOPY,)),
            dma((NCOPY,)),
            dma((2, 19)),
            dma((2, 19)),
            dma((8,)),
        ],
        compiler_params=pltpu.CompilerParams(
            collective_id=0, has_side_effects=True, vmem_limit_bytes=60 * 2**20
        ),
    )(weights, history, inverse_blocks, incident, *tables)


def per_device(
    weights, history, send_patch, send_lag, send_class, recv_target,
    local_src, local_lag, local_class, local_target, inverse_blocks, incident,
):
    return near_field(
        weights, history, inverse_blocks, incident,
        (send_patch.T, send_lag.T, send_class.T, recv_target.T, local_src, local_lag, local_class, local_target),
    )


def solution(mesh):
    both = ("grp", "lag")
    return jax.shard_map(
        per_device,
        mesh=mesh,
        in_specs=(
            P(None, "lag", None), P(both, None, None),
            P(both, None), P(both, None), P(both, None), P(both, None),
            P(both), P(both), P(both), P(both),
            P(both, None, None), P(both, None, None),
        ),
        out_specs=P(both, None, None),
        check_vma=False,
    )
```
